512 devices in a mesh: row: 16 (over x, y_hi, core), col: 32 (over y_lo, z).
Axes of the slice: x: 4, y: 4 (y_hi: 2, y_lo: 2; y = y_hi * 2 + y_lo), z: 16, core: 2. Of those that a mesh axis runs over, the one named last changes fastest.
Arguments:
- contact: bfloat16 [1024, 65536], P('row', 'col'), may hold values from -6 to 6
- first_down: bfloat16 [2, 3, 3, 32, 64], replicated, may hold values from -0.25 to 0.25
- first_down_bias: float32 [2, 32], replicated, may hold values from -1.5 to 1.5
- first_up: bfloat16 [2, 3, 3, 64, 32], replicated, may hold values from -0.375 to 0.375
- first_up_bias: float32 [2, 64], replicated, may hold values from -1.5 to 1.5
- second_down: bfloat16 [2, 3, 3, 32, 64], replicated, may hold values from -0.25 to 0.25
- second_down_bias: float32 [2, 32], replicated, may hold values from -1.5 to 1.5
- second_up: bfloat16 [2, 3, 3, 64, 32], replicated, may hold values from -0.375 to 0.375
- second_up_bias: float32 [2, 64], replicated, may hold values from -1.5 to 1.5
Outputs:
- decoded: bfloat16 [1024, 65536], P('row', 'col')
The draws below stay inside these ranges and needn't reach their ends.
All inputs are finite; a program needn't handle non-finite values.
Results may differ from the reference program's by a relative error of at most 0.012.
Values may be sent and summed in bfloat16 or wider, within the bound.
No kernel may reach another device: no remote copies, remote signals or barrier semaphores. Data moves between devices by JAX's collectives and lax.ppermute only.
A program may use at most 64 MiB of HBM per device.

```python
import jax
import jax.numpy as jnp
from jax import lax

C = 64
CI = 32
H = 1024
W = 1024


def shard_levels(key, dims, pieces, low, high):
    gain, own = 1.0, jax.random.fold_in(key, 6)
    for axis_at, shards_of in pieces:
        heights = jnp.exp(jax.random.uniform(jax.random.fold_in(own, axis_at), (shards_of,), jnp.float32, low / len(pieces), high / len(pieces)))
        gain = gain * jnp.repeat(heights, dims[axis_at] // shards_of).reshape([-1 if axis == axis_at else 1 for axis in range(len(dims))])
    return gain


def normal_values(key, dims, scale, reach, shards=(), held_as=jnp.bfloat16):
    values = jax.random.normal(key, dims, jnp.float32) * scale
    if len(shards) > 0:
        values = shard_levels(key, dims, shards, -0.22, 0.18) * values
    return jnp.clip(values, min=-reach, max=reach).astype(held_as)


def setup_inputs(seed: int = 0) -> dict:
    splits = jax.random.split(jax.random.key(seed), 10)
    contact = normal_values(splits[0], (H, W * C), 1.0, 6.0, ((0, 16), (1, 32)))
    first_down = normal_values(splits[1], (2, 3, 3, CI, C), (9 * C) ** -0.5, 0.25)
    first_down_bias = normal_values(splits[2], (2, CI), 0.3, 1.5, (), jnp.float32)
    first_up = normal_values(splits[3], (2, 3, 3, C, CI), (9 * CI) ** -0.5, 0.375)
    first_up_bias = normal_values(splits[4], (2, C), 0.3, 1.5, (), jnp.float32)
    second_down = normal_values(splits[5], (2, 3, 3, CI, C), (9 * C) ** -0.5, 0.25)
    second_down_bias = normal_values(splits[6], (2, CI), 0.3, 1.5, (), jnp.float32)
    second_up = normal_values(splits[7], (2, 3, 3, C, CI), (9 * CI) ** -0.5, 0.375)
    second_up_bias = normal_values(splits[8], (2, C), 0.3, 1.5, (), jnp.float32)
    return {"contact": contact, "first_down": first_down, "first_down_bias": first_down_bias, "first_up": first_up, "first_up_bias": first_up_bias, "second_down": second_down, "second_down_bias": second_down_bias, "second_up": second_up, "second_up_bias": second_up_bias}


def convolve(field, weight, bias_term, dilation):
    result = lax.conv_general_dilated(
        field.astype(jnp.float32)[None],
        weight.astype(jnp.float32).transpose(2, 3, 0, 1),
        (1, 1),
        [(dilation, dilation), (dilation, dilation)],
        rhs_dilation=(dilation, dilation),
        dimension_numbers=("NCHW", "OIHW", "NCHW"),
        precision=lax.Precision.HIGHEST,
    )[0]
    return result + bias_term[:, None, None]


def run_section(field, down_weight, down_bias, up_weight, up_bias):
    for block_index, dilations in enumerate(((1, 2), (4, 8))):
        hidden = jax.nn.relu(convolve(field, down_weight[block_index], down_bias[block_index], dilations[0])).astype(jnp.bfloat16)
        update = convolve(hidden, up_weight[block_index], up_bias[block_index], dilations[1])
        field = (field.astype(jnp.float32) + update).astype(jnp.bfloat16)
    return field


def reference(contact, first_down, first_down_bias, first_up, first_up_bias, second_down, second_down_bias, second_up, second_up_bias):
    field = contact.reshape(H, W, C).transpose(2, 0, 1)
    first = run_section(field, first_down, first_down_bias, first_up, first_up_bias)
    widened = first.astype(jnp.float32)
    symmetric = ((widened + widened.transpose(0, 2, 1)) * 0.5).astype(jnp.bfloat16)
    result = run_section(symmetric, second_down, second_down_bias, second_up, second_up_bias)
    return result.transpose(1, 2, 0).reshape(H, W * C)
```

```python
import functools

import jax
import jax.numpy as jnp
from jax import lax
from jax.experimental import pallas as pl
from jax.experimental.pallas import tpu as pltpu
from jax.sharding import PartitionSpec as P

ROWS = 64
COLS = 32
CH = 64
HALO = 16
TALL = ROWS + 2 * HALO
F32 = jnp.float32
BF16 = jnp.bfloat16


def lane_group(width, rows):
    return lax.broadcasted_iota(jnp.int32, (rows, 128), 1) // width


def build_weights(down, up, w1, w2, w3, w4):
    by32 = lane_group(32, 64)
    by64 = lane_group(64, 32)
    zero_down = jnp.zeros((64, 128), BF16)
    zero_up = jnp.zeros((32, 128), BF16)
    for p in range(3):
        for i in range(8):
            block = zero_down
            for q in range(3):
                o = i - 1 - q
                if 0 <= o < 4:
                    block = jnp.where(by32 == o, down[0, p, q], block)
            w1[i * 64 : (i + 1) * 64, p * 128 : (p + 1) * 128] = block
        for i in range(8):
            for half in range(2):
                block = zero_up
                for q in range(3):
                    o = i - 2 * q
                    if 0 <= o < 4 and o // 2 == half:
                        block = jnp.where(by64 == o % 2, up[0, p, q], block)
                w2[i * 32 : (i + 1) * 32, p * 256 + half * 128 : p * 256 + half * 128 + 128] = block
        for t in range(4):
            for e in range(2):
                block = zero_down
                for u in range(2):
                    q = t - u
                    if 0 <= q < 3:
                        block = jnp.where(by32 == 2 * u + e, down[1, p, q], block)
                w3[t * 128 + e * 64 : t * 128 + e * 64 + 64, p * 128 : (p + 1) * 128] = block
        for q in range(3):
            for g in range(4):
                for half in range(2):
                    block = zero_up
                    if g // 2 == half:
                        block = jnp.where(by64 == g % 2, up[1, p, q], block)
                    w4[
                        q * 128 + g * 32 : q * 128 + g * 32 + 32,
                        p * 256 + half * 128 : p * 256 + half * 128 + 128,
                    ] = block


def section_kernel(
    size, at, own, left, right, above, below, down, down_bias, up, up_bias, out,
    v, h1, h2, w1, w2, w3, w4, row_mask
):
    build_weights(down, up, w1, w2, w3, w4)
    row0, col0 = at[0], at[1]
    height, width = size

    rows = row0 + lax.broadcasted_iota(jnp.int32, (TALL, 128), 0)
    row_mask[...] = ((rows >= 0) & (rows < height)).astype(F32)
    v[0] = jnp.zeros((TALL, 128), BF16)
    v[33] = jnp.zeros((TALL, 128), BF16)
    for i in range(32):
        lanes = slice(i * 128, (i + 1) * 128)
        v[i + 1, 0:HALO, :] = above[:, lanes]
        v[i + 1, HALO + ROWS : TALL, :] = below[:, lanes]
        if i < 8:
            middle = left[:, lanes]
        elif i < 24:
            middle = own[:, (i - 8) * 128 : (i - 7) * 128]
        else:
            middle = right[:, (i - 24) * 128 : (i - 23) * 128]
        v[i + 1, HALO : HALO + ROWS, :] = middle

    lane32 = lane_group(32, 1)
    lane64 = lane_group(64, 1)

    def col_mask(cols):
        return ((cols >= 0) & (cols < width)).astype(F32)

    def wide_dot(chunks, w):
        lhs = jnp.concatenate([jnp.concatenate(c, axis=0) for c in chunks], axis=1)
        return jnp.dot(lhs, w[...], preferred_element_type=F32)

    def taps(res, g, d, lo, n):
        part = res[g * TALL : (g + 1) * TALL]
        top = part[:, lo : lo + 128]
        mid = part[:, n + lo : n + lo + 128]
        low = part[:, 2 * n + lo : 2 * n + lo + 128]
        return pltpu.roll(top, d, 0) + mid + pltpu.roll(low, TALL - d, 0)

    def first_down(jj, _):
        j0 = jj * 4
        res = wide_dot([[v[2 * (j0 + g) + t] for g in range(4)] for t in range(4)], w1)
        for g in range(4):
            hidden = jnp.maximum(taps(res, g, 1, 0, 128) + down_bias[0:1], 0.0)
            keep = col_mask(col0 + 4 * (j0 + g) + lane32)
            h1[j0 + g] = (hidden * row_mask[...] * keep).astype(BF16)
        return 0

    lax.fori_loop(0, 4, first_down, 0)

    def first_up(kk, _):
        k0 = kk * 3
        res = wide_dot([[h1[k0 + g + t] for g in range(3)] for t in range(2)], w2)
        for g in range(3):
            for half in range(2):
                i = 2 * (k0 + g) + 1 + half
                update = taps(res, g, 2, half * 128, 256) + up_bias[0:1]
                value = (v[i + 1].astype(F32) + update) * row_mask[...]
                v[i + 1] = (value * col_mask(col0 + 2 * i + lane64)).astype(BF16)
        return 0

    lax.fori_loop(0, 5, first_up, 0)

    def second_down(mm, _):
        groups = [(1 + 2 * mm + dm, s) for dm in range(2) for s in range(2)]
        res = wide_dot([[v[4 * m + s - 1 + 2 * t] for m, s in groups] for t in range(4)], w3)
        for g, (m, s) in enumerate(groups):
            hidden = jnp.maximum(taps(res, g, 4, 0, 128) + down_bias[1:2], 0.0)
            keep = col_mask(col0 + 8 * m + 2 * s + 4 * (lane32 // 2) + lane32 % 2)
            h2[2 * (m - 1) + s] = (hidden * row_mask[...] * keep).astype(BF16)
        return 0

    lax.fori_loop(0, 3, second_down, 0)

    def second_up(mm, _):
        groups = [(2 + 2 * mm + dm, s) for dm in range(2) for s in range(2)]
        res = wide_dot([[h2[2 * (m - 2 + q) + s] for m, s in groups] for q in range(3)], w4)
        for g, (m, s) in enumerate(groups):
            base = g * TALL
            for half in range(2):
                lo = half * 128
                update = (
                    res[base + 8 : base + 72, lo : lo + 128]
                    + res[base + 16 : base + 80, 256 + lo : 384 + lo]
                    + res[base + 24 : base + 88, 512 + lo : 640 + lo]
                    + up_bias[1:2]
                )
                i = 4 * m + s + 2 * half
                value = v[i + 1][HALO : HALO + ROWS].astype(F32) + update
                at_lane = pl.multiple_of((i - 8) * 128, 128)
                out[:, pl.ds(at_lane, 128)] = value.astype(BF16)
        return 0

    lax.fori_loop(0, 2, second_up, 0)


def section(size, at, pieces, down, down_bias, up, up_bias):
    vmem = pl.BlockSpec(memory_space=pltpu.VMEM)
    return pl.pallas_call(
        functools.partial(section_kernel, size),
        out_shape=jax.ShapeDtypeStruct((ROWS, COLS * CH), BF16),
        in_specs=[pl.BlockSpec(memory_space=pltpu.SMEM)] + [vmem] * 9,
        out_specs=vmem,
        scratch_shapes=[
            pltpu.VMEM((34, TALL, 128), BF16),
            pltpu.VMEM((16, TALL, 128), BF16),
            pltpu.VMEM((12, TALL, 128), BF16),
            pltpu.VMEM((512, 384), BF16),
            pltpu.VMEM((256, 768), BF16),
            pltpu.VMEM((512, 384), BF16),
            pltpu.VMEM((384, 768), BF16),
            pltpu.VMEM((TALL, 128), F32),
        ],
        compiler_params=pltpu.CompilerParams(vmem_limit_bytes=32 << 20),
    )(at, *pieces, down, down_bias, up, up_bias)


def solution(mesh):
    row_count, col_count = mesh.shape["row"], mesh.shape["col"]
    size = (row_count * ROWS, col_count * COLS)
    flip = row_count // 4
    axes = ("row", "col")

    def send(x, target):
        pairs = []
        for r in range(row_count):
            for c in range(col_count):
                to = target(r, c)
                if 0 <= to[0] < row_count and 0 <= to[1] < col_count:
                    pairs.append((r * col_count + c, to[0] * col_count + to[1]))
        return lax.ppermute(x, axes, pairs)

    def with_rim(x):
        depth = HALO * CH
        right = send(x[:, :depth], lambda r, c: (r, c - 1))
        left = send(x[:, -depth:], lambda r, c: (r, c + 1))
        wide = jnp.concatenate([left[:HALO], x[:HALO], right[:HALO]], axis=1)
        wide_low = jnp.concatenate([left[-HALO:], x[-HALO:], right[-HALO:]], axis=1)
        below = send(wide, lambda r, c: (r - 1, c))
        above = send(wide_low, lambda r, c: (r + 1, c))
        return x, left, right, above, below

    def mirrored(x, parity):
        turned = x.reshape(2, 32, 32, CH).transpose(0, 2, 1, 3).reshape(2, 32, 32 * CH)
        near = lax.dynamic_index_in_dim(turned, parity, 0, keepdims=False)
        far = lax.dynamic_index_in_dim(turned, 1 - parity, 0, keepdims=False)
        far = send(far, lambda r, c: (r ^ flip, c))
        near = send(near, lambda r, c: (c // 2, 2 * r + c % 2))
        far = send(far, lambda r, c: (c // 2, 2 * (r ^ flip) + 1 - c % 2))
        even = jnp.concatenate([near, far], axis=0)
        odd = jnp.concatenate([far, near], axis=0)
        return jnp.where(parity == 0, even, odd)

    def per_device(contact, d1, db1, u1, ub1, d2, db2, u2, ub2):
        row, col = lax.axis_index("row"), lax.axis_index("col")
        at = jnp.stack([row * ROWS - HALO, col * COLS - HALO]).astype(jnp.int32)

        def prepared(down, down_bias, up, up_bias):
            return (
                jnp.tile(down.transpose(0, 1, 2, 4, 3), (1, 1, 1, 1, 4)),
                jnp.tile(down_bias, (1, 4)),
                jnp.tile(up.transpose(0, 1, 2, 4, 3), (1, 1, 1, 1, 2)),
                jnp.tile(up_bias, (1, 2)),
            )

        first = section(size, at, with_rim(contact), *prepared(d1, db1, u1, ub1))
        flipped = mirrored(first, col % 2)
        symmetric = ((first.astype(F32) + flipped.astype(F32)) * 0.5).astype(BF16)
        return section(size, at, with_rim(symmetric), *prepared(d2, db2, u2, ub2))

    in_specs = (P("row", "col"), P(), P(), P(), P(), P(), P(), P(), P())
    return jax.shard_map(
        per_device, mesh=mesh, in_specs=in_specs, out_specs=P("row", "col"), check_vma=False
    )
```

```python
import functools

import jax
import jax.numpy as jnp
from jax import lax
from jax.experimental import pallas as pl
from jax.experimental.pallas import tpu as pltpu
from jax.sharding import PartitionSpec as P

ROWS = 64
COLS = 32
CH = 64
HALO = 16
TALL = ROWS + 2 * HALO
F32 = jnp.float32
BF16 = jnp.bfloat16


def lane_group(width, rows):
    return lax.broadcasted_iota(jnp.int32, (rows, 128), 1) // width


def build_weights(down, up, w1, w2, w3, w4):
    by32 = lane_group(32, 64)
    by64 = lane_group(64, 32)
    zero_down = jnp.zeros((64, 128), BF16)
    zero_up = jnp.zeros((32, 128), BF16)
    for p in range(3):
        for i in range(8):
            block = zero_down
            for q in range(3):
                o = i - 1 - q
                if 0 <= o < 4:
                    block = jnp.where(by32 == o, down[0, p, q], block)
            w1[i * 64 : (i + 1) * 64, p * 128 : (p + 1) * 128] = block
        for i in range(8):
            for half in range(2):
                block = zero_up
                for q in range(3):
                    o = i - 2 * q
                    if 0 <= o < 4 and o // 2 == half:
                        block = jnp.where(by64 == o % 2, up[0, p, q], block)
                w2[i * 32 : (i + 1) * 32, half * 384 + p * 128 : half * 384 + p * 128 + 128] = block
        for t in range(4):
            for e in range(2):
                block = zero_down
                for u in range(2):
                    q = t - u
                    if 0 <= q < 3:
                        block = jnp.where(by32 == 2 * u + e, down[1, p, q], block)
                w3[t * 128 + e * 64 : t * 128 + e * 64 + 64, p * 128 : (p + 1) * 128] = block
        for q in range(3):
            for g in range(4):
                for half in range(2):
                    block = zero_up
                    if g // 2 == half:
                        block = jnp.where(by64 == g % 2, up[1, p, q], block)
                    w4[
                        q * 128 + g * 32 : q * 128 + g * 32 + 32,
                        p * 256 + half * 128 : p * 256 + half * 128 + 128,
                    ] = block


def section_kernel(
    spots, bars, at, *refs
):
    pieces, refs = refs[: len(spots)], refs[len(spots) :]
    down, down_bias, up, up_bias, out, v, h1, h2, w1, w2, w3, w4 = refs
    build_weights(down, up, w1, w2, w3, w4)
    low_col, high_col, cut_low, cut_high = at[0], at[1], at[2], at[3]
    low_row, high_row = bars

    nothing = jnp.zeros((TALL, 128), BF16)
    v[0] = nothing
    v[33] = nothing
    h1[16] = nothing
    h2[12] = nothing
    for piece, (row, pair) in zip(pieces, spots):
        for i in range(piece.shape[1] // 128):
            v[pair + i + 1, row : row + piece.shape[0], :] = piece[:, i * 128 : (i + 1) * 128]

    sub = lax.broadcasted_iota(jnp.int32, (8, 128), 0)

    def cut(d):
        keep_top = jnp.where((sub >= 8 - d) & (cut_low > 0), 0.0, 1.0)
        keep_low = jnp.where((sub < d) & (cut_high > 0), 0.0, 1.0)
        return keep_top, keep_low

    def wide_dot(chunks, w, lo, hi):
        lhs = jnp.concatenate([jnp.concatenate(c, axis=0) for c in chunks], axis=1)
        return jnp.dot(lhs, w[:, lo:hi], preferred_element_type=F32)

    def parts(res, g, keep, lo, n):
        part = res[g * TALL : (g + 1) * TALL]
        top = part[:, lo : lo + 128]
        mid = part[:, n + lo : n + lo + 128]
        low = part[:, 2 * n + lo : 2 * n + lo + 128]
        top = jnp.concatenate(
            [top[: low_row - 8], top[low_row - 8 : low_row] * keep[0], top[low_row:]], axis=0
        )
        low = jnp.concatenate(
            [low[:high_row], low[high_row : high_row + 8] * keep[1], low[high_row + 8 :]], axis=0
        )
        return top, mid, low

    def taps(res, g, d, keep, lo, n):
        top, mid, low = parts(res, g, keep, lo, n)
        return pltpu.roll(top, d, 0) + mid + pltpu.roll(low, TALL - d, 0)

    def first_down(jj, _):
        j0 = jj * 4
        keep = cut(1)

        def pair_of(j, t):
            if t == 0:
                return jnp.where(j == 2 * low_col, 33, 2 * j)
            if t == 3:
                return jnp.where(j == 2 * high_col - 1, 33, 2 * j + 3)
            return 2 * j + t

        chunks = [[v[pair_of(j0 + g, t)] for g in range(4)] for t in range(4)]
        res = wide_dot(chunks, w1, 0, 384)
        for g in range(4):
            hidden = jnp.maximum(taps(res, g, 1, keep, 0, 128) + down_bias[0:1], 0.0)
            h1[j0 + g] = hidden.astype(BF16)
        return 0

    lax.fori_loop(0, 4, first_down, 0)

    def first_up(kk, _):
        k0 = kk * 3
        keep = cut(2)
        for half in range(2):
            hidden = []
            for g in range(3):
                k = k0 + g
                near, far = k, k + 1
                if half == 0:
                    far = jnp.where(far == 2 * high_col, 16, far)
                else:
                    near = jnp.where(far == 2 * low_col, 16, near)
                hidden.append((near, far))
            chunks = [[h1[pair[t]] for pair in hidden] for t in range(2)]
            res = wide_dot(chunks, w2, half * 384, half * 384 + 384)
            for g in range(3):
                i = 2 * (k0 + g) + 1 + half
                update = taps(res, g, 2, keep, 0, 128) + up_bias[0:1]
                v[i + 1] = (v[i + 1].astype(F32) + update).astype(BF16)
        return 0

    lax.fori_loop(0, 5, first_up, 0)

    def second_down(mm, _):
        groups = [(1 + 2 * mm + dm, s) for dm in range(2) for s in range(2)]
        keep = cut(4)

        def pair_of(m, s, t):
            if t == 0:
                return jnp.where(m == low_col, 33, 4 * m + s - 1)
            if t == 3:
                return jnp.where(m == high_col - 1, 33, 4 * m + s + 5)
            return 4 * m + s - 1 + 2 * t

        res = wide_dot([[v[pair_of(m, s, t)] for m, s in groups] for t in range(4)], w3, 0, 384)
        for g, (m, s) in enumerate(groups):
            hidden = jnp.maximum(taps(res, g, 4, keep, 0, 128) + down_bias[1:2], 0.0)
            h2[2 * (m - 1) + s] = hidden.astype(BF16)
        return 0

    lax.fori_loop(0, 3, second_down, 0)

    def second_up(mm, _):
        groups = [(2 + 2 * mm + dm, s) for dm in range(2) for s in range(2)]
        keep = cut(8)

        def group_of(m, s, q):
            if q == 0:
                return jnp.where(m == low_col, 12, 2 * (m - 2) + s)
            if q == 2:
                return jnp.where(m == high_col - 1, 12, 2 * m + s)
            return 2 * (m - 1) + s

        res = wide_dot([[h2[group_of(m, s, q)] for m, s in groups] for q in range(3)], w4, 0, 768)
        for g, (m, s) in enumerate(groups):
            for half in range(2):
                top, mid, low = parts(res, g, keep, half * 128, 256)
                update = top[8:72] + mid[16:80] + low[24:88] + up_bias[1:2]
                i = 4 * m + s + 2 * half
                value = v[i + 1][HALO : HALO + ROWS].astype(F32) + update
                at_lane = pl.multiple_of((i - 8) * 128, 128)
                out[:, pl.ds(at_lane, 128)] = value.astype(BF16)
        return 0

    lax.fori_loop(0, 2, second_up, 0)


def section(spots, bars, at, pieces, down, down_bias, up, up_bias):
    vmem = pl.BlockSpec(memory_space=pltpu.VMEM)
    return pl.pallas_call(
        functools.partial(section_kernel, spots, bars),
        out_shape=jax.ShapeDtypeStruct((ROWS, COLS * CH), BF16),
        in_specs=[pl.BlockSpec(memory_space=pltpu.SMEM)] + [vmem] * (len(spots) + 4),
        out_specs=vmem,
        scratch_shapes=[
            pltpu.VMEM((34, TALL, 128), BF16),
            pltpu.VMEM((17, TALL, 128), BF16),
            pltpu.VMEM((13, TALL, 128), BF16),
            pltpu.VMEM((512, 384), BF16),
            pltpu.VMEM((256, 768), BF16),
            pltpu.VMEM((512, 384), BF16),
            pltpu.VMEM((384, 768), BF16),
        ],
        compiler_params=pltpu.CompilerParams(vmem_limit_bytes=32 << 20),
    )(at, *pieces, down, down_bias, up, up_bias)


AHEAD = ((0, 0), (0, 16), (64, 0), (64, 16))
BEHIND = ((32, 16), (32, 0), (0, 16), (0, 0))


def solution(mesh):
    row_count, col_count = mesh.shape["row"], mesh.shape["col"]
    flip = row_count // 4
    axes = ("row", "col")

    def send(x, target):
        pairs = []
        for r in range(row_count):
            for c in range(col_count):
                row, col = target(r, c)
                to = (row % row_count) * col_count + col % col_count
                pairs.append((r * col_count + c, to))
        return lax.ppermute(x, axes, pairs)

    def with_ahead(x):
        corner = send(x[:32], lambda r, c: (r - 1, c - 1))
        right = send(x, lambda r, c: (r, c - 1))
        below = send(x[:32], lambda r, c: (r - 1, c))
        return x, right, below, corner

    def with_behind(x):
        corner = send(x[32:], lambda r, c: (r + 1, c + 1))
        left = send(x, lambda r, c: (r, c + 1))
        above = send(x[32:], lambda r, c: (r + 1, c))
        return x, left, above, corner

    def mirrored(x, parity):
        turned = x.reshape(2, 32, 32, CH).transpose(0, 2, 1, 3).reshape(2, 32, 32 * CH)
        near = lax.dynamic_index_in_dim(turned, parity, 0, keepdims=False)
        far = lax.dynamic_index_in_dim(turned, 1 - parity, 0, keepdims=False)
        far = send(far, lambda r, c: (r ^ flip, c))
        near = send(near, lambda r, c: (c // 2, 2 * r + c % 2))
        far = send(far, lambda r, c: (c // 2, 2 * (r ^ flip) + 1 - c % 2))
        even = jnp.concatenate([near, far], axis=0)
        odd = jnp.concatenate([far, near], axis=0)
        return jnp.where(parity == 0, even, odd)

    def per_device(contact, d1, db1, u1, ub1, d2, db2, u2, ub2):
        row, col = lax.axis_index("row"), lax.axis_index("col")
        first_row, last_row = row == 0, row == row_count - 1
        first_col, last_col = col == 0, col == col_count - 1

        def flags(low_at, low_col, high_at, high_col, low_row, high_row):
            return jnp.stack(
                [
                    jnp.where(low_col, low_at, -1),
                    jnp.where(high_col, high_at, -1),
                    low_row.astype(jnp.int32),
                    high_row.astype(jnp.int32),
                ]
            ).astype(jnp.int32)

        def prepared(down, down_bias, up, up_bias):
            return (
                jnp.tile(down.transpose(0, 1, 2, 4, 3), (1, 1, 1, 1, 4)),
                jnp.tile(down_bias, (1, 4)),
                jnp.tile(up.transpose(0, 1, 2, 4, 3), (1, 1, 1, 1, 2)),
                jnp.tile(up_bias, (1, 2)),
            )

        at = flags(4, last_col, 4, last_col, last_row, last_row)
        first = section(AHEAD, (64, 64), at, with_ahead(contact), *prepared(d1, db1, u1, ub1))
        flipped = mirrored(first, col % 2)
        symmetric = ((first.astype(F32) + flipped.astype(F32)) * 0.5).astype(BF16)
        at = flags(2, first_col, 6, last_col, first_row, last_row)
        return section(BEHIND, (16, 80), at, with_behind(symmetric), *prepared(d2, db2, u2, ub2))

    in_specs = (P("row", "col"), P(), P(), P(), P(), P(), P(), P(), P())
    return jax.shard_map(
        per_device, mesh=mesh, in_specs=in_specs, out_specs=P("row", "col"), check_vma=False
    )
```

```python
import functools

import jax
import jax.numpy as jnp
from jax import lax
from jax.experimental import pallas as pl
from jax.experimental.pallas import tpu as pltpu
from jax.sharding import PartitionSpec as P

ROWS = 64
COLS = 32
CH = 64
HALO = 16
TALL = ROWS + 2 * HALO
F32 = jnp.float32
BF16 = jnp.bfloat16


def lane_group(width, rows):
    return lax.broadcasted_iota(jnp.int32, (rows, 128), 1) // width


def build_weights(down, up, w1, w2, w3, w4):
    by32 = lane_group(32, 64)
    by64 = lane_group(64, 32)
    zero_down = jnp.zeros((64, 128), BF16)
    zero_up = jnp.zeros((32, 128), BF16)
    for p in range(3):
        for i in range(8):
            block = zero_down
            for q in range(3):
                o = i - 1 - q
                if 0 <= o < 4:
                    block = jnp.where(by32 == o, down[0, p, q], block)
            w1[i * 64 : (i + 1) * 64, p * 128 : (p + 1) * 128] = block
        for i in range(8):
            for half in range(2):
                block = zero_up
                for q in range(3):
                    o = i - 2 * q
                    if 0 <= o < 4 and o // 2 == half:
                        block = jnp.where(by64 == o % 2, up[0, p, q], block)
                w2[i * 32 : (i + 1) * 32, half * 384 + p * 128 : half * 384 + p * 128 + 128] = block
        for t in range(4):
            for e in range(2):
                block = zero_down
                for u in range(2):
                    q = t - u
                    if 0 <= q < 3:
                        block = jnp.where(by32 == 2 * u + e, down[1, p, q], block)
                w3[t * 128 + e * 64 : t * 128 + e * 64 + 64, p * 128 : (p + 1) * 128] = block
        for q in range(3):
            for g in range(4):
                for half in range(2):
                    block = zero_up
                    if g // 2 == half:
                        block = jnp.where(by64 == g % 2, up[1, p, q], block)
                    w4[
                        q * 128 + g * 32 : q * 128 + g * 32 + 32,
                        p * 256 + half * 128 : p * 256 + half * 128 + 128,
                    ] = block


def section_kernel(
    spots, bars, turn, at, *refs
):
    pieces, refs = refs[: len(spots)], refs[len(spots) :]
    w1, w2, w3, w4, down_bias, up_bias, out = refs[:7]
    turning = turn and refs[7:10]
    v, h1, h2 = refs[-3:]
    low_col, high_col, cut_low, cut_high = at[0], at[1], at[2], at[3]
    low_row, high_row = bars

    nothing = jnp.zeros((TALL, 128), BF16)
    v[0] = nothing
    v[33] = nothing
    h1[16] = nothing
    h2[12] = nothing
    for piece, (row, pair) in zip(pieces, spots):
        for i in range(piece.shape[1] // 128):
            v[pair + i + 1, row : row + piece.shape[0], :] = piece[:, i * 128 : (i + 1) * 128]

    sub = lax.broadcasted_iota(jnp.int32, (8, 128), 0)

    def cut(d):
        keep_top = jnp.where((sub >= 8 - d) & (cut_low > 0), 0.0, 1.0)
        keep_low = jnp.where((sub < d) & (cut_high > 0), 0.0, 1.0)
        return keep_top, keep_low

    def wide_dot(chunks, w, lo, hi):
        lhs = jnp.concatenate([jnp.concatenate(c, axis=0) for c in chunks], axis=1)
        return jnp.dot(lhs, w[:, lo:hi], preferred_element_type=F32)

    def parts(res, g, keep, lo, n):
        part = res[g * TALL : (g + 1) * TALL]
        top = part[:, lo : lo + 128]
        mid = part[:, n + lo : n + lo + 128]
        low = part[:, 2 * n + lo : 2 * n + lo + 128]
        top = jnp.concatenate(
            [top[: low_row - 8], top[low_row - 8 : low_row] * keep[0], top[low_row:]], axis=0
        )
        low = jnp.concatenate(
            [low[:high_row], low[high_row : high_row + 8] * keep[1], low[high_row + 8 :]], axis=0
        )
        return top, mid, low

    def taps(res, g, d, keep, lo, n):
        top, mid, low = parts(res, g, keep, lo, n)
        return pltpu.roll(top, d, 0) + mid + pltpu.roll(low, TALL - d, 0)

    def first_down(jj, _):
        j0 = jj * 4
        keep = cut(1)

        def pair_of(j, t):
            if t == 0:
                return jnp.where(j == 2 * low_col, 33, 2 * j)
            if t == 3:
                return jnp.where(j == 2 * high_col - 1, 33, 2 * j + 3)
            return 2 * j + t

        chunks = [[v[pair_of(j0 + g, t)] for g in range(4)] for t in range(4)]
        res = wide_dot(chunks, w1, 0, 384)
        for g in range(4):
            hidden = jnp.maximum(taps(res, g, 1, keep, 0, 128) + down_bias[0:1], 0.0)
            h1[j0 + g] = hidden.astype(BF16)
        return 0

    lax.fori_loop(0, 4, first_down, 0)

    def first_up(kk, _):
        k0 = kk * 3
        keep = cut(2)
        for half in range(2):
            hidden = []
            for g in range(3):
                k = k0 + g
                near, far = k, k + 1
                if half == 0:
                    far = jnp.where(far == 2 * high_col, 16, far)
                else:
                    near = jnp.where(far == 2 * low_col, 16, near)
                hidden.append((near, far))
            chunks = [[h1[pair[t]] for pair in hidden] for t in range(2)]
            res = wide_dot(chunks, w2, half * 384, half * 384 + 384)
            for g in range(3):
                i = 2 * (k0 + g) + 1 + half
                update = taps(res, g, 2, keep, 0, 128) + up_bias[0:1]
                v[i + 1] = (v[i + 1].astype(F32) + update).astype(BF16)
        return 0

    lax.fori_loop(0, 5, first_up, 0)

    def second_down(mm, _):
        groups = [(1 + 2 * mm + dm, s) for dm in range(2) for s in range(2)]
        keep = cut(4)

        def pair_of(m, s, t):
            if t == 0:
                return jnp.where(m == low_col, 33, 4 * m + s - 1)
            if t == 3:
                return jnp.where(m == high_col - 1, 33, 4 * m + s + 5)
            return 4 * m + s - 1 + 2 * t

        res = wide_dot([[v[pair_of(m, s, t)] for m, s in groups] for t in range(4)], w3, 0, 384)
        for g, (m, s) in enumerate(groups):
            hidden = jnp.maximum(taps(res, g, 4, keep, 0, 128) + down_bias[1:2], 0.0)
            h2[2 * (m - 1) + s] = hidden.astype(BF16)
        return 0

    lax.fori_loop(0, 3, second_down, 0)

    def second_up(mm, _):
        groups = [(2 + 2 * mm + dm, s) for dm in range(2) for s in range(2)]
        keep = cut(8)

        def group_of(m, s, q):
            if q == 0:
                return jnp.where(m == low_col, 12, 2 * (m - 2) + s)
            if q == 2:
                return jnp.where(m == high_col - 1, 12, 2 * m + s)
            return 2 * (m - 1) + s

        res = wide_dot([[h2[group_of(m, s, q)] for m, s in groups] for q in range(3)], w4, 0, 768)
        for g, (m, s) in enumerate(groups):
            for half in range(2):
                top, mid, low = parts(res, g, keep, half * 128, 256)
                update = top[8:72] + mid[16:80] + low[24:88] + up_bias[1:2]
                i = 4 * m + s + 2 * half
                value = v[i + 1][HALO : HALO + ROWS].astype(F32) + update
                at_lane = pl.multiple_of((i - 8) * 128, 128)
                value = value.astype(BF16)
                out[:, pl.ds(at_lane, 128)] = value
                if turn:
                    value = value.astype(F32)
                    strip = pl.multiple_of((i - 8) * 128, 128)
                    turning[2][pl.ds(strip, 64), :] = value
                    turning[2][pl.ds(strip + 64, 64), :] = pltpu.roll(value, 64, 1)
        return 0

    lax.fori_loop(0, 2, second_up, 0)

    if turn:
        near, far, lines = turning
        left_half = lax.broadcasted_iota(jnp.int32, (32, 128), 1) < 64
        for target, base in ((near, at[4] * 32), (far, (1 - at[4]) * 32)):
            for j in range(16):
                even = lines[pl.ds(base + 2 * j, 32, stride=64), :]
                odd = lines[pl.ds(base + 2 * j + 1, 32, stride=64), :]
                both = jnp.where(left_half, even, pltpu.roll(odd, 64, 1))
                target[:, j * 128 : (j + 1) * 128] = both.astype(BF16)


def weights(down, up):
    vmem = pl.BlockSpec(memory_space=pltpu.VMEM)
    shapes = [(512, 384), (256, 768), (512, 384), (384, 768)]
    return pl.pallas_call(
        build_weights,
        out_shape=[jax.ShapeDtypeStruct(shape, BF16) for shape in shapes],
        in_specs=[vmem, vmem],
        out_specs=[vmem] * 4,
    )(down, up)


def section(spots, bars, turn, at, pieces, matrices, down_bias, up_bias):
    vmem = pl.BlockSpec(memory_space=pltpu.VMEM)
    out_shape = [jax.ShapeDtypeStruct((ROWS, COLS * CH), BF16)]
    scratch = [
        pltpu.VMEM((34, TALL, 128), BF16),
        pltpu.VMEM((17, TALL, 128), BF16),
        pltpu.VMEM((13, TALL, 128), BF16),
    ]
    if turn:
        out_shape += [jax.ShapeDtypeStruct((32, 32 * CH), BF16)] * 2
        scratch = [pltpu.VMEM((ROWS * COLS, 128), F32)] + scratch
    return pl.pallas_call(
        functools.partial(section_kernel, spots, bars, turn),
        out_shape=out_shape,
        in_specs=[pl.BlockSpec(memory_space=pltpu.SMEM)] + [vmem] * (len(spots) + 6),
        out_specs=[vmem] * len(out_shape),
        scratch_shapes=scratch,
        compiler_params=pltpu.CompilerParams(vmem_limit_bytes=32 << 20),
    )(at, *pieces, *matrices, down_bias, up_bias)


AHEAD = ((0, 0), (0, 16), (64, 0), (64, 16))
BEHIND = ((32, 16), (32, 0), (0, 16), (0, 0))


def solution(mesh):
    row_count, col_count = mesh.shape["row"], mesh.shape["col"]
    flip = row_count // 4
    axes = ("row", "col")

    def send(x, target):
        pairs = []
        for r in range(row_count):
            for c in range(col_count):
                row, col = target(r, c)
                to = (row % row_count) * col_count + col % col_count
                pairs.append((r * col_count + c, to))
        return lax.ppermute(x, axes, pairs)

    def with_ahead(x):
        corner = send(x[:32], lambda r, c: (r - 1, c - 1))
        right = send(x, lambda r, c: (r, c - 1))
        below = send(x[:32], lambda r, c: (r - 1, c))
        return x, right, below, corner

    def with_behind(x):
        corner = send(x[32:], lambda r, c: (r + 1, c + 1))
        left = send(x, lambda r, c: (r, c + 1))
        above = send(x[32:], lambda r, c: (r + 1, c))
        return x, left, above, corner

    def mirrored(near, far, parity):
        far = send(far, lambda r, c: (r ^ flip, c))
        near = send(near, lambda r, c: (c // 2, 2 * r + c % 2))
        far = send(far, lambda r, c: (c // 2, 2 * (r ^ flip) + 1 - c % 2))
        even = jnp.concatenate([near, far], axis=0)
        odd = jnp.concatenate([far, near], axis=0)
        return jnp.where(parity == 0, even, odd)

    def per_device(contact, d1, db1, u1, ub1, d2, db2, u2, ub2):
        row, col = lax.axis_index("row"), lax.axis_index("col")
        first_row, last_row = row == 0, row == row_count - 1
        first_col, last_col = col == 0, col == col_count - 1

        def flags(low_at, low_col, high_at, high_col, low_row, high_row):
            return jnp.stack(
                [
                    jnp.where(low_col, low_at, -1),
                    jnp.where(high_col, high_at, -1),
                    low_row.astype(jnp.int32),
                    high_row.astype(jnp.int32),
                    col % 2,
                ]
            ).astype(jnp.int32)

        def matrices(down, up):
            return weights(
                jnp.tile(down.transpose(0, 1, 2, 4, 3), (1, 1, 1, 1, 4)),
                jnp.tile(up.transpose(0, 1, 2, 4, 3), (1, 1, 1, 1, 2)),
            )

        def biases(down_bias, up_bias):
            return jnp.tile(down_bias, (1, 4)), jnp.tile(up_bias, (1, 2))

        at = flags(4, last_col, 4, last_col, last_row, last_row)
        pieces = with_ahead(contact)
        first, near, far = section(
            AHEAD, (64, 64), True, at, pieces, matrices(d1, u1), *biases(db1, ub1)
        )
        later = matrices(d2, u2)
        flipped = mirrored(near, far, col % 2)
        symmetric = ((first.astype(F32) + flipped.astype(F32)) * 0.5).astype(BF16)
        symmetric, later = lax.optimization_barrier((symmetric, later))
        at = flags(2, first_col, 6, last_col, first_row, last_row)
        return section(
            BEHIND, (16, 80), False, at, with_behind(symmetric), later, *biases(db2, ub2)
        )[0]

    in_specs = (P("row", "col"), P(), P(), P(), P(), P(), P(), P(), P())
    return jax.shard_map(
        per_device, mesh=mesh, in_specs=in_specs, out_specs=P("row", "col"), check_vma=False
    )
```

```python
import functools

import jax
import jax.numpy as jnp
from jax import lax
from jax.experimental import pallas as pl
from jax.experimental.pallas import tpu as pltpu
from jax.sharding import PartitionSpec as P

ROWS = 64
COLS = 32
CH = 64
HALO = 16
TALL = ROWS + 2 * HALO
F32 = jnp.float32
BF16 = jnp.bfloat16


def lane_group(width, rows):
    return lax.broadcasted_iota(jnp.int32, (rows, 128), 1) // width


def build_weights(down, up, w1, w2, w3, w4):
    by32 = lane_group(32, 64)
    by64 = lane_group(64, 32)
    zero_down = jnp.zeros((64, 128), BF16)
    zero_up = jnp.zeros((32, 128), BF16)
    for p in range(3):
        for i in range(8):
            block = zero_down
            for q in range(3):
                o = i - 1 - q
                if 0 <= o < 4:
                    block = jnp.where(by32 == o, down[0, p, q], block)
            w1[i * 64 : (i + 1) * 64, p * 128 : (p + 1) * 128] = block
        for i in range(8):
            for half in range(2):
                block = zero_up
                for q in range(3):
                    o = i - 2 * q
                    if 0 <= o < 4 and o // 2 == half:
                        block = jnp.where(by64 == o % 2, up[0, p, q], block)
                w2[i * 32 : (i + 1) * 32, half * 384 + p * 128 : half * 384 + p * 128 + 128] = block
        for t in range(4):
            for e in range(2):
                block = zero_down
                for u in range(2):
                    q = t - u
                    if 0 <= q < 3:
                        block = jnp.where(by32 == 2 * u + e, down[1, p, q], block)
                w3[t * 128 + e * 64 : t * 128 + e * 64 + 64, p * 128 : (p + 1) * 128] = block
        for q in range(3):
            for g in range(4):
                for half in range(2):
                    block = zero_up
                    if g // 2 == half:
                        block = jnp.where(by64 == g % 2, up[1, p, q], block)
                    w4[
                        q * 128 + g * 32 : q * 128 + g * 32 + 32,
                        p * 256 + half * 128 : p * 256 + half * 128 + 128,
                    ] = block


def section_kernel(
    spots, bars, turn, at, *refs
):
    pieces, refs = refs[: len(spots)], refs[len(spots) :]
    w1, w2, w3, w4, down_bias, up_bias, out = refs[:7]
    turning = turn and refs[7:10]
    v, h1, h2 = refs[-3:]
    low_col, high_col, cut_low, cut_high = at[0], at[1], at[2], at[3]
    low_row, high_row = bars

    nothing = jnp.zeros((TALL, 128), BF16)
    v[0] = nothing
    v[33] = nothing
    h1[16] = nothing
    h2[12] = nothing
    for piece, (row, pair) in zip(pieces, spots):
        for i in range(piece.shape[1] // 128):
            v[pair + i + 1, row : row + piece.shape[0], :] = piece[:, i * 128 : (i + 1) * 128]

    sub = lax.broadcasted_iota(jnp.int32, (8, 128), 0)

    def cut(d):
        keep_top = jnp.where((sub >= 8 - d) & (cut_low > 0), 0.0, 1.0)
        keep_low = jnp.where((sub < d) & (cut_high > 0), 0.0, 1.0)
        return keep_top, keep_low

    def wide_dot(chunks, w, lo, hi):
        lhs = jnp.concatenate([jnp.concatenate(c, axis=0) for c in chunks], axis=1)
        return jnp.dot(lhs, w[:, lo:hi], preferred_element_type=F32)

    def parts(res, g, keep, lo, n):
        part = res[g * TALL : (g + 1) * TALL]
        top = part[:, lo : lo + 128]
        mid = part[:, n + lo : n + lo + 128]
        low = part[:, 2 * n + lo : 2 * n + lo + 128]
        top = jnp.concatenate(
            [top[: low_row - 8], top[low_row - 8 : low_row] * keep[0], top[low_row:]], axis=0
        )
        low = jnp.concatenate(
            [low[:high_row], low[high_row : high_row + 8] * keep[1], low[high_row + 8 :]], axis=0
        )
        return top, mid, low

    def taps(res, g, d, keep, lo, n):
        top, mid, low = parts(res, g, keep, lo, n)
        return pltpu.roll(top, d, 0) + mid + pltpu.roll(low, TALL - d, 0)

    def first_down(jj, _):
        j0 = jj * 4
        keep = cut(1)

        def pair_of(j, t):
            if t == 0:
                return jnp.where(j == 2 * low_col, 33, 2 * j)
            if t == 3:
                return jnp.where(j == 2 * high_col - 1, 33, 2 * j + 3)
            return 2 * j + t

        chunks = [[v[pair_of(j0 + g, t)] for g in range(4)] for t in range(4)]
        res = wide_dot(chunks, w1, 0, 384)
        for g in range(4):
            hidden = jnp.maximum(taps(res, g, 1, keep, 0, 128) + down_bias[0:1], 0.0)
            h1[j0 + g] = hidden.astype(BF16)
        return 0

    lax.fori_loop(0, 4, first_down, 0)

    def first_up(kk, _):
        k0 = kk * 3
        keep = cut(2)
        for half in range(2):
            hidden = []
            for g in range(3):
                k = k0 + g
                near, far = k, k + 1
                if half == 0:
                    far = jnp.where(far == 2 * high_col, 16, far)
                else:
                    near = jnp.where(far == 2 * low_col, 16, near)
                hidden.append((near, far))
            chunks = [[h1[pair[t]] for pair in hidden] for t in range(2)]
            res = wide_dot(chunks, w2, half * 384, half * 384 + 384)
            for g in range(3):
                i = 2 * (k0 + g) + 1 + half
                update = taps(res, g, 2, keep, 0, 128) + up_bias[0:1]
                v[i + 1] = (v[i + 1].astype(F32) + update).astype(BF16)
        return 0

    lax.fori_loop(0, 5, first_up, 0)

    def second_down(mm, _):
        groups = [(1 + 2 * mm + dm, s) for dm in range(2) for s in range(2)]
        keep = cut(4)

        def pair_of(m, s, t):
            if t == 0:
                return jnp.where(m == low_col, 33, 4 * m + s - 1)
            if t == 3:
                return jnp.where(m == high_col - 1, 33, 4 * m + s + 5)
            return 4 * m + s - 1 + 2 * t

        res = wide_dot([[v[pair_of(m, s, t)] for m, s in groups] for t in range(4)], w3, 0, 384)
        for g, (m, s) in enumerate(groups):
            hidden = jnp.maximum(taps(res, g, 4, keep, 0, 128) + down_bias[1:2], 0.0)
            h2[2 * (m - 1) + s] = hidden.astype(BF16)
        return 0

    lax.fori_loop(0, 3, second_down, 0)

    def second_up(mm, _):
        groups = [(2 + 2 * mm + dm, s) for dm in range(2) for s in range(2)]
        keep = cut(8)

        def group_of(m, s, q):
            if q == 0:
                return jnp.where(m == low_col, 12, 2 * (m - 2) + s)
            if q == 2:
                return jnp.where(m == high_col - 1, 12, 2 * m + s)
            return 2 * (m - 1) + s

        res = wide_dot([[h2[group_of(m, s, q)] for m, s in groups] for q in range(3)], w4, 0, 768)
        for g, (m, s) in enumerate(groups):
            for half in range(2):
                top, mid, low = parts(res, g, keep, half * 128, 256)
                update = top[8:72] + mid[16:80] + low[24:88] + up_bias[1:2]
                i = 4 * m + s + 2 * half
                value = v[i + 1][HALO : HALO + ROWS].astype(F32) + update
                at_lane = pl.multiple_of((i - 8) * 128, 128)
                value = value.astype(BF16)
                out[:, pl.ds(at_lane, 128)] = value
                if turn:
                    value = value.astype(F32)
                    strip = pl.multiple_of((i - 8) * 128, 128)
                    turning[2][pl.ds(strip, 64), :] = value
                    turning[2][pl.ds(strip + 64, 64), :] = pltpu.roll(value, 64, 1)
        return 0

    lax.fori_loop(0, 2, second_up, 0)

    if turn:
        near, far, lines = turning
        left_half = lax.broadcasted_iota(jnp.int32, (32, 128), 1) < 64
        for target, base in ((near, at[4] * 32), (far, (1 - at[4]) * 32)):
            for j in range(16):
                even = lines[pl.ds(base + 2 * j, 32, stride=64), :]
                odd = lines[pl.ds(base + 2 * j + 1, 32, stride=64), :]
                both = jnp.where(left_half, even, pltpu.roll(odd, 64, 1))
                target[:, j * 128 : (j + 1) * 128] = both.astype(BF16)


def weights(down, up):
    vmem = pl.BlockSpec(memory_space=pltpu.VMEM)
    shapes = [(512, 384), (256, 768), (512, 384), (384, 768)]
    return pl.pallas_call(
        build_weights,
        out_shape=[jax.ShapeDtypeStruct(shape, BF16) for shape in shapes],
        in_specs=[vmem, vmem],
        out_specs=[vmem] * 4,
        compiler_params=pltpu.CompilerParams(vmem_limit_bytes=8 << 20),
    )(down, up)


def section(spots, bars, turn, at, pieces, matrices, down_bias, up_bias):
    vmem = pl.BlockSpec(memory_space=pltpu.VMEM)
    out_shape = [jax.ShapeDtypeStruct((ROWS, COLS * CH), BF16)]
    scratch = [
        pltpu.VMEM((34, TALL, 128), BF16),
        pltpu.VMEM((17, TALL, 128), BF16),
        pltpu.VMEM((13, TALL, 128), BF16),
    ]
    if turn:
        out_shape += [jax.ShapeDtypeStruct((32, 32 * CH), BF16)] * 2
        scratch = [pltpu.VMEM((ROWS * COLS, 128), F32)] + scratch
    return pl.pallas_call(
        functools.partial(section_kernel, spots, bars, turn),
        out_shape=out_shape,
        in_specs=[pl.BlockSpec(memory_space=pltpu.SMEM)] + [vmem] * (len(spots) + 6),
        out_specs=[vmem] * len(out_shape),
        scratch_shapes=scratch,
        compiler_params=pltpu.CompilerParams(vmem_limit_bytes=16 << 20),
    )(at, *pieces, *matrices, down_bias, up_bias)


AHEAD = ((0, 0), (0, 16), (64, 0), (64, 16))
BEHIND = ((32, 16), (32, 0), (0, 16), (0, 0))


def solution(mesh):
    row_count, col_count = mesh.shape["row"], mesh.shape["col"]
    flip = row_count // 4
    axes = ("row", "col")

    def send(x, target):
        pairs = []
        for r in range(row_count):
            for c in range(col_count):
                row, col = target(r, c)
                to = (row % row_count) * col_count + col % col_count
                pairs.append((r * col_count + c, to))
        return lax.ppermute(x, axes, pairs)

    def with_ahead(x):
        corner = send(x[:32], lambda r, c: (r - 1, c - 1))
        right = send(x, lambda r, c: (r, c - 1))
        below = send(x[:32], lambda r, c: (r - 1, c))
        return x, right, below, corner

    def with_behind(x):
        corner = send(x[32:], lambda r, c: (r + 1, c + 1))
        left = send(x, lambda r, c: (r, c + 1))
        above = send(x[32:], lambda r, c: (r + 1, c))
        return x, left, above, corner

    def mirrored(near, far, parity):
        far = send(far, lambda r, c: (r ^ flip, c))
        near = send(near, lambda r, c: (c // 2, 2 * r + c % 2))
        far = send(far, lambda r, c: (c // 2, 2 * (r ^ flip) + 1 - c % 2))
        even = jnp.concatenate([near, far], axis=0)
        odd = jnp.concatenate([far, near], axis=0)
        return jnp.where(parity == 0, even, odd)

    def per_device(contact, d1, db1, u1, ub1, d2, db2, u2, ub2):
        row, col = lax.axis_index("row"), lax.axis_index("col")
        first_row, last_row = row == 0, row == row_count - 1
        first_col, last_col = col == 0, col == col_count - 1

        def flags(low_at, low_col, high_at, high_col, low_row, high_row):
            return jnp.stack(
                [
                    jnp.where(low_col, low_at, -1),
                    jnp.where(high_col, high_at, -1),
                    low_row.astype(jnp.int32),
                    high_row.astype(jnp.int32),
                    col % 2,
                ]
            ).astype(jnp.int32)

        def matrices(down, up):
            return weights(
                jnp.tile(down.transpose(0, 1, 2, 4, 3), (1, 1, 1, 1, 4)),
                jnp.tile(up.transpose(0, 1, 2, 4, 3), (1, 1, 1, 1, 2)),
            )

        def biases(down_bias, up_bias):
            return jnp.tile(down_bias, (1, 4)), jnp.tile(up_bias, (1, 2))

        at = flags(4, last_col, 4, last_col, last_row, last_row)
        pieces = with_ahead(contact)
        first, near, far = section(
            AHEAD, (64, 64), True, at, pieces, matrices(d1, u1), *biases(db1, ub1)
        )
        later = matrices(d2, u2)
        flipped = mirrored(near, far, col % 2)
        symmetric = ((first.astype(F32) + flipped.astype(F32)) * 0.5).astype(BF16)
        symmetric, later = lax.optimization_barrier((symmetric, later))
        at = flags(2, first_col, 6, last_col, first_row, last_row)
        return section(
            BEHIND, (16, 80), False, at, with_behind(symmetric), later, *biases(db2, ub2)
        )[0]

    in_specs = (P("row", "col"), P(), P(), P(), P(), P(), P(), P(), P())
    return jax.shard_map(
        per_device, mesh=mesh, in_specs=in_specs, out_specs=P("row", "col"), check_vma=False
    )
```

```python
import functools

import jax
import jax.numpy as jnp
from jax import lax
from jax.experimental import pallas as pl
from jax.experimental.pallas import tpu as pltpu
from jax.sharding import PartitionSpec as P

ROWS = 64
COLS = 32
CH = 64
HALO = 16
TALL = ROWS + 2 * HALO
MID = 80
F32 = jnp.float32
BF16 = jnp.bfloat16


def lane_group(width, rows):
    return lax.broadcasted_iota(jnp.int32, (rows, 128), 1) // width


def build_weights(down, up, w1, w2, w3, w4):
    by32 = lane_group(32, 64)
    by64 = lane_group(64, 32)
    zero_down = jnp.zeros((64, 128), BF16)
    zero_up = jnp.zeros((32, 128), BF16)
    for p in range(3):
        for i in range(8):
            block = zero_down
            for q in range(3):
                o = i - 1 - q
                if 0 <= o < 4:
                    block = jnp.where(by32 == o, down[0, p, q], block)
            w1[i * 64 : (i + 1) * 64, p * 128 : (p + 1) * 128] = block
        for i in range(8):
            for half in range(2):
                block = zero_up
                for q in range(3):
                    o = i - 2 * q
                    if 0 <= o < 4 and o // 2 == half:
                        block = jnp.where(by64 == o % 2, up[0, p, q], block)
                w2[i * 32 : (i + 1) * 32, half * 384 + p * 128 : half * 384 + p * 128 + 128] = block
        for t in range(4):
            for e in range(2):
                block = zero_down
                for u in range(2):
                    q = t - u
                    if 0 <= q < 3:
                        block = jnp.where(by32 == 2 * u + e, down[1, p, q], block)
                w3[t * 128 + e * 64 : t * 128 + e * 64 + 64, p * 128 : (p + 1) * 128] = block
        for q in range(3):
            for e in range(2):
                block = jnp.where(by64 == e, up[1, p, q], zero_up)
                w4[q * 64 + e * 32 : q * 64 + e * 32 + 32, p * 128 : (p + 1) * 128] = block
        w4[192:256, p * 128 : (p + 1) * 128] = zero_down


def turn_strips(values, halves, row):
    sub = lax.broadcasted_iota(jnp.int32, (8, 128), 0)
    left = lax.broadcasted_iota(jnp.int32, (8, 128), 1) < 64

    def swapped(x, one, other, bit):
        a, b = x[one], x[other]
        low = (sub & bit) == 0
        x[one] = jnp.where(low, a, pltpu.roll(b, bit, 0))
        x[other] = jnp.where(low, pltpu.roll(a, 8 - bit, 0), b)

    for block in range(8):
        x = [values[i][8 * block : 8 * block + 8] for i in range(4)]
        swapped(x, 0, 1, 2)
        swapped(x, 2, 3, 2)
        swapped(x, 0, 2, 4)
        swapped(x, 1, 3, 4)
        for j in range(4):
            z = pltpu.roll(x[j], 64, 1)
            even = jnp.where(left, x[j], pltpu.roll(z, 7, 0))
            odd = jnp.where(left, pltpu.roll(z, 1, 0), x[j])
            both = jnp.where((sub & 1) == 0, even, odd).astype(BF16)
            lane = (4 * block + j) % 16 * 128
            halves[block // 4][row : row + 8, lane : lane + 128] = both


def section_kernel(
    spots, bars, turn, at, *refs
):
    pieces, refs = refs[: len(spots)], refs[len(spots) :]
    w1, w2, w3, w4, down_bias, up_bias, out = refs[:7]
    turning = turn and refs[7:9]
    v, h1, h2, h2_turned = refs[-4:]
    low_on, high_on, cut_low, cut_high = at[0] > 0, at[1] > 0, at[2], at[3]
    low_row, high_row, low_col, high_col = bars

    nothing = jnp.zeros((TALL, 128), BF16)
    v[0] = nothing
    v[33] = nothing
    h1[16] = nothing
    h2[12] = nothing[:MID]
    h2_turned[12] = nothing[:MID]
    for piece, (row, pair) in zip(pieces, spots):
        for i in range(piece.shape[1] // 128):
            v[pair + i + 1, row : row + piece.shape[0], :] = piece[:, i * 128 : (i + 1) * 128]

    sub = lax.broadcasted_iota(jnp.int32, (8, 128), 0)

    def cut(d):
        keep_top = jnp.where((sub >= 8 - d) & (cut_low > 0), 0.0, 1.0)
        keep_low = jnp.where((sub < d) & (cut_high > 0), 0.0, 1.0)
        return keep_top, keep_low

    def wide_dot(chunks, w):
        lhs = jnp.concatenate([jnp.concatenate(c, axis=0) for c in chunks], axis=1)
        return jnp.dot(lhs, w[...], preferred_element_type=F32)

    def masked(x, start, keep):
        pieces = [x[:start], x[start : start + 8] * keep, x[start + 8 :]]
        return jnp.concatenate([p for p in pieces if p.shape[0]], axis=0)

    def parts(part, keep, lo, off):
        top = masked(part[:, lo : lo + 128], low_row - 8 - off, keep[0])
        mid = part[:, lo + 128 : lo + 256]
        low = masked(part[:, lo + 256 : lo + 384], high_row - off, keep[1])
        return top, mid, low

    def taps(res, g, d, keep, lo):
        top, mid, low = parts(res[g * TALL : (g + 1) * TALL], keep, lo, 0)
        return pltpu.roll(top, d, 0) + mid + pltpu.roll(low, TALL - d, 0)

    def below_bar(hit, index, blank):
        return jnp.where(low_on, blank, index) if hit else index

    def above_bar(hit, index, blank):
        return jnp.where(high_on, blank, index) if hit else index

    keep = cut(1)
    for j0 in range(0, 16, 4):
        quads = range(j0, j0 + 4)
        res = wide_dot(
            [
                [v[below_bar(j == 2 * low_col, 2 * j, 33)] for j in quads],
                [v[2 * j + 1] for j in quads],
                [v[2 * j + 2] for j in quads],
                [v[above_bar(j == 2 * high_col - 1, 2 * j + 3, 33)] for j in quads],
            ],
            w1,
        )
        for g, j in enumerate(quads):
            hidden = jnp.maximum(taps(res, g, 1, keep, 0) + down_bias[0:1], 0.0)
            h1[j] = hidden.astype(BF16)

    keep = cut(2)
    steps = []
    for k in range(15):
        near = below_bar(k + 1 == 2 * low_col, k, 16)
        far = above_bar(k + 1 == 2 * high_col, k + 1, 16)
        if k + 1 == 2 * low_col == 2 * high_col:
            steps += [(k, k, far, (0,)), (k, near, k + 1, (1,))]
        else:
            steps.append((k, near, far, (0, 1)))
    for at_step in range(0, len(steps), 4):
        some = steps[at_step : at_step + 4]
        res = wide_dot([[h1[step[1]] for step in some], [h1[step[2]] for step in some]], w2)
        for g, (k, _, _, halves) in enumerate(some):
            for half in halves:
                i = 2 * k + 1 + half
                update = taps(res, g, 2, keep, half * 384) + up_bias[0:1]
                v[i + 1] = (v[i + 1].astype(F32) + update).astype(BF16)

    keep = cut(4)
    for m0 in range(1, 7, 2):
        groups = [(m0 + dm, s) for dm in range(2) for s in range(2)]
        res = wide_dot(
            [
                [v[below_bar(m == low_col, 4 * m + s - 1, 33)] for m, s in groups],
                [v[4 * m + s + 1] for m, s in groups],
                [v[4 * m + s + 3] for m, s in groups],
                [v[above_bar(m == high_col - 1, 4 * m + s + 5, 33)] for m, s in groups],
            ],
            w3,
        )
        for g, (m, s) in enumerate(groups):
            hidden = jnp.maximum(taps(res, g, 4, keep, 0) + down_bias[1:2], 0.0)
            hidden = hidden[8 : 8 + MID]
            h2[2 * (m - 1) + s] = hidden.astype(BF16)
            h2_turned[2 * (m - 1) + s] = pltpu.roll(hidden, 64, 1).astype(BF16)

    keep = cut(8)
    first_half = lax.broadcasted_iota(jnp.int32, (MID, 128), 1) < 64
    for m in range(2, 6):
        groups = [(s, u) for s in range(2) for u in range(2)]
        chunks = [[], []]
        for s, u in groups:
            straight, turned = (h2, h2_turned) if u == 0 else (h2_turned, h2)
            before = below_bar(m == low_col, 2 * (m - 2) + s, 12)
            after = above_bar(m == high_col - 1, 2 * m + s, 12)
            here = 2 * (m - 1) + s
            chunks[0].append(jnp.where(first_half, straight[before], turned[here]))
            chunks[1].append(straight[after])
        res = wide_dot(chunks, w4)
        values = {}
        for g, (s, u) in enumerate(groups):
            top, mid, low = parts(res[g * MID : (g + 1) * MID], keep, 0, 8)
            update = top[0:64] + mid[8:72] + low[16:80] + up_bias[1:2]
            i = 4 * m + s + 2 * u
            value = v[i + 1][HALO : HALO + ROWS].astype(F32) + update
            strip = (i - 8) * 128
            value = value.astype(BF16)
            out[:, strip : strip + 128] = value
            values[s + 2 * u] = value.astype(F32)
        if turn:
            turn_strips(values, turning, 8 * (m - 2))


def weights(down, up):
    vmem = pl.BlockSpec(memory_space=pltpu.VMEM)
    shapes = [(512, 384), (256, 768), (512, 384), (256, 384)]
    return pl.pallas_call(
        build_weights,
        out_shape=[jax.ShapeDtypeStruct(shape, BF16) for shape in shapes],
        in_specs=[vmem, vmem],
        out_specs=[vmem] * 4,
        compiler_params=pltpu.CompilerParams(vmem_limit_bytes=8 << 20),
    )(down, up)


def section(spots, bars, turn, at, pieces, matrices, down_bias, up_bias):
    vmem = pl.BlockSpec(memory_space=pltpu.VMEM)
    out_shape = [jax.ShapeDtypeStruct((ROWS, COLS * CH), BF16)]
    scratch = [
        pltpu.VMEM((34, TALL, 128), BF16),
        pltpu.VMEM((17, TALL, 128), BF16),
        pltpu.VMEM((13, MID, 128), BF16),
        pltpu.VMEM((13, MID, 128), BF16),
    ]
    if turn:
        out_shape += [jax.ShapeDtypeStruct((32, 32 * CH), BF16)] * 2
    return pl.pallas_call(
        functools.partial(section_kernel, spots, bars, turn),
        out_shape=out_shape,
        in_specs=[pl.BlockSpec(memory_space=pltpu.SMEM)] + [vmem] * (len(spots) + 6),
        out_specs=[vmem] * len(out_shape),
        scratch_shapes=scratch,
        compiler_params=pltpu.CompilerParams(vmem_limit_bytes=16 << 20),
    )(at, *pieces, *matrices, down_bias, up_bias)


AHEAD = ((0, 0), (0, 16), (64, 0), (64, 16))
BEHIND = ((32, 16), (32, 0), (0, 16), (0, 0))


def solution(mesh):
    row_count, col_count = mesh.shape["row"], mesh.shape["col"]
    flip = row_count // 4
    axes = ("row", "col")

    def send(x, target):
        pairs = []
        for r in range(row_count):
            for c in range(col_count):
                row, col = target(r, c)
                to = (row % row_count) * col_count + col % col_count
                pairs.append((r * col_count + c, to))
        return lax.ppermute(x, axes, pairs)

    def with_ahead(x):
        corner = send(x[:32], lambda r, c: (r - 1, c - 1))
        right = send(x, lambda r, c: (r, c - 1))
        below = send(x[:32], lambda r, c: (r - 1, c))
        return x, right, below, corner

    def with_behind(x):
        corner = send(x[32:], lambda r, c: (r + 1, c + 1))
        left = send(x, lambda r, c: (r, c + 1))
        above = send(x[32:], lambda r, c: (r + 1, c))
        return x, left, above, corner

    def mirrored(top, bottom, parity):
        near = jnp.where(parity == 0, top, bottom)
        far = jnp.where(parity == 0, bottom, top)
        far = send(far, lambda r, c: (r ^ flip, c))
        near = send(near, lambda r, c: (c // 2, 2 * r + c % 2))
        far = send(far, lambda r, c: (c // 2, 2 * (r ^ flip) + 1 - c % 2))
        even = jnp.concatenate([near, far], axis=0)
        odd = jnp.concatenate([far, near], axis=0)
        return jnp.where(parity == 0, even, odd)

    def per_device(contact, d1, db1, u1, ub1, d2, db2, u2, ub2):
        row, col = lax.axis_index("row"), lax.axis_index("col")
        first_row, last_row = row == 0, row == row_count - 1
        first_col, last_col = col == 0, col == col_count - 1

        def flags(low_at, low_col, high_at, high_col, low_row, high_row):
            return jnp.stack(
                [
                    jnp.where(low_col, low_at, -1),
                    jnp.where(high_col, high_at, -1),
                    low_row.astype(jnp.int32),
                    high_row.astype(jnp.int32),
                ]
            ).astype(jnp.int32)

        def matrices(down, up):
            return weights(
                jnp.tile(down.transpose(0, 1, 2, 4, 3), (1, 1, 1, 1, 4)),
                jnp.tile(up.transpose(0, 1, 2, 4, 3), (1, 1, 1, 1, 2)),
            )

        def biases(down_bias, up_bias):
            return jnp.tile(down_bias, (1, 4)), jnp.tile(up_bias, (1, 2))

        at = flags(4, last_col, 4, last_col, last_row, last_row)
        pieces = with_ahead(contact)
        first, top, bottom = section(
            AHEAD, (64, 64, 4, 4), True, at, pieces, matrices(d1, u1), *biases(db1, ub1)
        )
        later = matrices(d2, u2)
        flipped = mirrored(top, bottom, col % 2)
        symmetric = ((first.astype(F32) + flipped.astype(F32)) * 0.5).astype(BF16)
        symmetric, later = lax.optimization_barrier((symmetric, later))
        at = flags(2, first_col, 6, last_col, first_row, last_row)
        return section(
            BEHIND, (16, 80, 2, 6), False, at, with_behind(symmetric), later, *biases(db2, ub2)
        )[0]

    in_specs = (P("row", "col"), P(), P(), P(), P(), P(), P(), P(), P())
    return jax.shard_map(
        per_device, mesh=mesh, in_specs=in_specs, out_specs=P("row", "col"), check_vma=False
    )
```

```python
import functools

import jax
import jax.numpy as jnp
from jax import lax
from jax.experimental import pallas as pl
from jax.experimental.pallas import tpu as pltpu
from jax.sharding import PartitionSpec as P

ROWS = 64
COLS = 32
CH = 64
HALO = 16
TALL = ROWS + 2 * HALO
MID = 80
F32 = jnp.float32
BF16 = jnp.bfloat16


def lane_group(width, rows):
    return lax.broadcasted_iota(jnp.int32, (rows, 128), 1) // width


def build_weights(down, up, w1, w2, w3, w4):
    by32 = lane_group(32, 64)
    by64 = lane_group(64, 32)
    zero_down = jnp.zeros((64, 128), BF16)
    zero_up = jnp.zeros((32, 128), BF16)
    for p in range(3):
        for i in range(8):
            block = zero_down
            for q in range(3):
                o = i - 1 - q
                if 0 <= o < 4:
                    block = jnp.where(by32 == o, down[0, p, q], block)
            w1[i * 64 : (i + 1) * 64, p * 128 : (p + 1) * 128] = block
        for i in range(8):
            for half in range(2):
                block = zero_up
                for q in range(3):
                    o = i - 2 * q
                    if 0 <= o < 4 and o // 2 == half:
                        block = jnp.where(by64 == o % 2, up[0, p, q], block)
                w2[i * 32 : (i + 1) * 32, half * 384 + p * 128 : half * 384 + p * 128 + 128] = block
        for t in range(4):
            for e in range(2):
                block = zero_down
                for u in range(2):
                    q = t - u
                    if 0 <= q < 3:
                        block = jnp.where(by32 == 2 * u + e, down[1, p, q], block)
                w3[t * 128 + e * 64 : t * 128 + e * 64 + 64, p * 128 : (p + 1) * 128] = block
        for q in range(3):
            for e in range(2):
                block = jnp.where(by64 == e, up[1, p, q], zero_up)
                w4[q * 64 + e * 32 : q * 64 + e * 32 + 32, p * 128 : (p + 1) * 128] = block
        w4[192:256, p * 128 : (p + 1) * 128] = zero_down


def turn_strips(values, halves, row):
    sub = lax.broadcasted_iota(jnp.int32, (8, 128), 0)
    left = lax.broadcasted_iota(jnp.int32, (8, 128), 1) < 64

    def swapped(x, one, other, bit):
        a, b = x[one], x[other]
        low = (sub & bit) == 0
        x[one] = jnp.where(low, a, pltpu.roll(b, bit, 0))
        x[other] = jnp.where(low, pltpu.roll(a, 8 - bit, 0), b)

    for block in range(8):
        x = [values[i][8 * block : 8 * block + 8] for i in range(4)]
        swapped(x, 0, 1, 2)
        swapped(x, 2, 3, 2)
        swapped(x, 0, 2, 4)
        swapped(x, 1, 3, 4)
        for j in range(4):
            z = pltpu.roll(x[j], 64, 1)
            even = jnp.where(left, x[j], pltpu.roll(z, 7, 0))
            odd = jnp.where(left, pltpu.roll(z, 1, 0), x[j])
            both = jnp.where((sub & 1) == 0, even, odd).astype(BF16)
            lane = (4 * block + j) % 16 * 128
            halves[block // 4][row : row + 8, lane : lane + 128] = both


def section_kernel(
    spots, bars, turn, at, *refs
):
    pieces, refs = refs[: len(spots)], refs[len(spots) :]
    w1, w2, w3, w4, down_bias, up_bias, out = refs[:7]
    turning = turn and refs[7:9]
    if not turn:
        result, out, sent = out, refs[7], refs[8]
        copies = []
    v, h1, h2, h2_turned = refs[-4:]
    low_on, high_on, cut_low, cut_high = at[0] > 0, at[1] > 0, at[2], at[3]
    low_row, high_row, low_col, high_col = bars

    nothing = jnp.zeros((TALL, 128), BF16)
    v[0] = nothing
    v[33] = nothing
    h1[16] = nothing
    h2[12] = nothing[:MID]
    h2_turned[12] = nothing[:MID]
    for piece, (row, pair) in zip(pieces, spots):
        for i in range(piece.shape[1] // 128):
            v[pair + i + 1, row : row + piece.shape[0], :] = piece[:, i * 128 : (i + 1) * 128]

    sub = lax.broadcasted_iota(jnp.int32, (8, 128), 0)

    def cut(d):
        keep_top = jnp.where((sub >= 8 - d) & (cut_low > 0), 0.0, 1.0)
        keep_low = jnp.where((sub < d) & (cut_high > 0), 0.0, 1.0)
        return keep_top, keep_low

    def wide_dot(chunks, w):
        lhs = jnp.concatenate([jnp.concatenate(c, axis=0) for c in chunks], axis=1)
        return jnp.dot(lhs, w[...], preferred_element_type=F32)

    def masked(x, start, keep):
        pieces = [x[:start], x[start : start + 8] * keep, x[start + 8 :]]
        return jnp.concatenate([p for p in pieces if p.shape[0]], axis=0)

    def parts(part, keep, lo, off):
        top = masked(part[:, lo : lo + 128], low_row - 8 - off, keep[0])
        mid = part[:, lo + 128 : lo + 256]
        low = masked(part[:, lo + 256 : lo + 384], high_row - off, keep[1])
        return top, mid, low

    def taps(res, g, d, keep, lo):
        top, mid, low = parts(res[g * TALL : (g + 1) * TALL], keep, lo, 0)
        return pltpu.roll(top, d, 0) + mid + pltpu.roll(low, TALL - d, 0)

    def below_bar(hit, index, blank):
        return jnp.where(low_on, blank, index) if hit else index

    def above_bar(hit, index, blank):
        return jnp.where(high_on, blank, index) if hit else index

    keep = cut(1)
    for j0 in range(0, 16, 4):
        quads = range(j0, j0 + 4)
        res = wide_dot(
            [
                [v[below_bar(j == 2 * low_col, 2 * j, 33)] for j in quads],
                [v[2 * j + 1] for j in quads],
                [v[2 * j + 2] for j in quads],
                [v[above_bar(j == 2 * high_col - 1, 2 * j + 3, 33)] for j in quads],
            ],
            w1,
        )
        for g, j in enumerate(quads):
            hidden = jnp.maximum(taps(res, g, 1, keep, 0) + down_bias[0:1], 0.0)
            h1[j] = hidden.astype(BF16)

    keep = cut(2)
    steps = []
    for k in range(15):
        near = below_bar(k + 1 == 2 * low_col, k, 16)
        far = above_bar(k + 1 == 2 * high_col, k + 1, 16)
        if k + 1 == 2 * low_col == 2 * high_col:
            steps += [(k, k, far, (0,)), (k, near, k + 1, (1,))]
        else:
            steps.append((k, near, far, (0, 1)))
    for at_step in range(0, len(steps), 4):
        some = steps[at_step : at_step + 4]
        res = wide_dot([[h1[step[1]] for step in some], [h1[step[2]] for step in some]], w2)
        for g, (k, _, _, halves) in enumerate(some):
            for half in halves:
                i = 2 * k + 1 + half
                update = taps(res, g, 2, keep, half * 384) + up_bias[0:1]
                v[i + 1] = (v[i + 1].astype(F32) + update).astype(BF16)

    keep = cut(4)
    for m0 in range(1, 7, 2):
        groups = [(m0 + dm, s) for dm in range(2) for s in range(2)]
        res = wide_dot(
            [
                [v[below_bar(m == low_col, 4 * m + s - 1, 33)] for m, s in groups],
                [v[4 * m + s + 1] for m, s in groups],
                [v[4 * m + s + 3] for m, s in groups],
                [v[above_bar(m == high_col - 1, 4 * m + s + 5, 33)] for m, s in groups],
            ],
            w3,
        )
        for g, (m, s) in enumerate(groups):
            hidden = jnp.maximum(taps(res, g, 4, keep, 0) + down_bias[1:2], 0.0)
            hidden = hidden[8 : 8 + MID]
            h2[2 * (m - 1) + s] = hidden.astype(BF16)
            h2_turned[2 * (m - 1) + s] = pltpu.roll(hidden, 64, 1).astype(BF16)

    keep = cut(8)
    first_half = lax.broadcasted_iota(jnp.int32, (MID, 128), 1) < 64
    for m in range(2, 6):
        groups = [(s, u) for s in range(2) for u in range(2)]
        chunks = [[], []]
        for s, u in groups:
            straight, turned = (h2, h2_turned) if u == 0 else (h2_turned, h2)
            before = below_bar(m == low_col, 2 * (m - 2) + s, 12)
            after = above_bar(m == high_col - 1, 2 * m + s, 12)
            here = 2 * (m - 1) + s
            chunks[0].append(jnp.where(first_half, straight[before], turned[here]))
            chunks[1].append(straight[after])
        res = wide_dot(chunks, w4)
        values = {}
        for g, (s, u) in enumerate(groups):
            top, mid, low = parts(res[g * MID : (g + 1) * MID], keep, 0, 8)
            update = top[0:64] + mid[8:72] + low[16:80] + up_bias[1:2]
            i = 4 * m + s + 2 * u
            value = v[i + 1][HALO : HALO + ROWS].astype(F32) + update
            strip = (i - 8) * 128
            value = value.astype(BF16)
            out[:, strip : strip + 128] = value
            values[s + 2 * u] = value.astype(F32)
        if turn:
            turn_strips(values, turning, 8 * (m - 2))
        else:
            lanes = slice((m - 2) * 512, (m - 1) * 512)
            copies.append(
                pltpu.make_async_copy(out.at[:, lanes], result.at[:, lanes], sent.at[m - 2])
            )
            copies[-1].start()

    if not turn:
        for copy in copies:
            copy.wait()


def weights(down, up):
    vmem = pl.BlockSpec(memory_space=pltpu.VMEM)
    shapes = [(512, 384), (256, 768), (512, 384), (256, 384)]
    return pl.pallas_call(
        build_weights,
        out_shape=[jax.ShapeDtypeStruct(shape, BF16) for shape in shapes],
        in_specs=[vmem, vmem],
        out_specs=[vmem] * 4,
        compiler_params=pltpu.CompilerParams(vmem_limit_bytes=8 << 20),
    )(down, up)


def section(spots, bars, turn, at, pieces, matrices, down_bias, up_bias):
    vmem = pl.BlockSpec(memory_space=pltpu.VMEM)
    out_shape = [jax.ShapeDtypeStruct((ROWS, COLS * CH), BF16)]
    scratch = [
        pltpu.VMEM((34, TALL, 128), BF16),
        pltpu.VMEM((17, TALL, 128), BF16),
        pltpu.VMEM((13, MID, 128), BF16),
        pltpu.VMEM((13, MID, 128), BF16),
    ]
    if turn:
        out_shape += [jax.ShapeDtypeStruct((32, 32 * CH), BF16)] * 2
    else:
        scratch = [pltpu.VMEM((ROWS, COLS * CH), BF16), pltpu.SemaphoreType.DMA((4,))] + scratch
    return pl.pallas_call(
        functools.partial(section_kernel, spots, bars, turn),
        out_shape=out_shape,
        in_specs=[pl.BlockSpec(memory_space=pltpu.SMEM)] + [vmem] * (len(spots) + 6),
        out_specs=[vmem] * 3 if turn else [pl.BlockSpec(memory_space=pl.ANY)],
        scratch_shapes=scratch,
        compiler_params=pltpu.CompilerParams(vmem_limit_bytes=16 << 20),
    )(at, *pieces, *matrices, down_bias, up_bias)


AHEAD = ((0, 0), (0, 16), (64, 0), (64, 16))
BEHIND = ((32, 16), (32, 0), (0, 16), (0, 0))


def solution(mesh):
    row_count, col_count = mesh.shape["row"], mesh.shape["col"]
    flip = row_count // 4
    axes = ("row", "col")

    def send(x, target):
        pairs = []
        for r in range(row_count):
            for c in range(col_count):
                row, col = target(r, c)
                to = (row % row_count) * col_count + col % col_count
                pairs.append((r * col_count + c, to))
        return lax.ppermute(x, axes, pairs)

    def with_ahead(x):
        corner = send(x[:32], lambda r, c: (r - 1, c - 1))
        right = send(x, lambda r, c: (r, c - 1))
        below = send(x[:32], lambda r, c: (r - 1, c))
        return x, right, below, corner

    def with_behind(x):
        corner = send(x[32:], lambda r, c: (r + 1, c + 1))
        left = send(x, lambda r, c: (r, c + 1))
        above = send(x[32:], lambda r, c: (r + 1, c))
        return x, left, above, corner

    def mirrored(top, bottom, parity):
        near = jnp.where(parity == 0, top, bottom)
        far = jnp.where(parity == 0, bottom, top)
        far = send(far, lambda r, c: (r ^ flip, c))
        near = send(near, lambda r, c: (c // 2, 2 * r + c % 2))
        far = send(far, lambda r, c: (c // 2, 2 * (r ^ flip) + 1 - c % 2))
        even = jnp.concatenate([near, far], axis=0)
        odd = jnp.concatenate([far, near], axis=0)
        return jnp.where(parity == 0, even, odd)

    def per_device(contact, d1, db1, u1, ub1, d2, db2, u2, ub2):
        row, col = lax.axis_index("row"), lax.axis_index("col")
        first_row, last_row = row == 0, row == row_count - 1
        first_col, last_col = col == 0, col == col_count - 1

        def flags(low_at, low_col, high_at, high_col, low_row, high_row):
            return jnp.stack(
                [
                    jnp.where(low_col, low_at, -1),
                    jnp.where(high_col, high_at, -1),
                    low_row.astype(jnp.int32),
                    high_row.astype(jnp.int32),
                ]
            ).astype(jnp.int32)

        def matrices(down, up):
            return weights(
                jnp.tile(down.transpose(0, 1, 2, 4, 3), (1, 1, 1, 1, 4)),
                jnp.tile(up.transpose(0, 1, 2, 4, 3), (1, 1, 1, 1, 2)),
            )

        def biases(down_bias, up_bias):
            return jnp.tile(down_bias, (1, 4)), jnp.tile(up_bias, (1, 2))

        at = flags(4, last_col, 4, last_col, last_row, last_row)
        pieces = with_ahead(contact)
        first, top, bottom = section(
            AHEAD, (64, 64, 4, 4), True, at, pieces, matrices(d1, u1), *biases(db1, ub1)
        )
        later = matrices(d2, u2)
        flipped = mirrored(top, bottom, col % 2)
        symmetric = ((first.astype(F32) + flipped.astype(F32)) * 0.5).astype(BF16)
        symmetric, later = lax.optimization_barrier((symmetric, later))
        at = flags(2, first_col, 6, last_col, first_row, last_row)
        return section(
            BEHIND, (16, 80, 2, 6), False, at, with_behind(symmetric), later, *biases(db2, ub2)
        )[0]

    in_specs = (P("row", "col"), P(), P(), P(), P(), P(), P(), P(), P())
    return jax.shard_map(
        per_device, mesh=mesh, in_specs=in_specs, out_specs=P("row", "col"), check_vma=False
    )
```
